32 devices in a mesh: grp: 2 (over y), row: 4 (over z), col: 4 (over x, core).
Axes of the slice: x: 2, y: 2, z: 4, core: 2. Of those that a mesh axis runs over, the one named last changes fastest.
Arguments:
- sky_cube: bfloat16 [1024, 512, 512], P(('grp', 'row'), 'col'), parts along dimension 0, may hold values from -40 to 40
- half_widths: int32 [512], replicated, may hold values from 1 to 16, as said below
- pixel_mask: int32 [1024, 512], P(('grp', 'row'), 'col'), parts along dimension 0, may hold values 0 or 1
- foreground_modes: float32 [32, 512], P('grp'), parts along dimension 0, may hold values from -6 to 6
Outputs:
- spectrum: float32 [512, 2, 512, 512], P(('grp', 'row', 'col')), parts along dimension 0
- channel_weights: float32 [1024], P('grp'), parts along dimension 0
The draws below stay inside these ranges and needn't reach their ends.
There are 2 independent parts, one for each index of `grp`. The reference program is written for one: setup_inputs(seed, part) draws one part's arguments, and reference() takes and returns one part's arrays. A program takes and returns all parts, laid end to end along the dimension named above; an argument that names none is the same for every part. Nothing has to cross between parts.
Inputs may be any that keep to these rules, and one draw needn't show every extreme that they name: `half_widths`: some channel has half-width exactly 16 and some exactly 1.
All inputs are finite; a program needn't handle non-finite values. No bound on the sum of `pixel_mask` on one device may be relied on, other than what follows from the above.
Results may differ from the reference program's by a relative error of at most 0.0087.
Values may be sent and summed in bfloat16 or wider, within the bound.
A program may use at most 192 MiB of HBM per device.

```python
import math
import jax
import jax.numpy as jnp
from jax import lax

NR = 512
NC = 512
NF = 512
NMODE = 16
HALF = 16


def sky_modes(key):
    mode_key = jax.random.fold_in(key, 11)
    drawn = jax.random.normal(mode_key, (NMODE, NF), jnp.float32)
    return jnp.clip(drawn, -6.0, 6.0)


def draw_foreground_modes(key, part):
    return sky_modes(key)


def diffuse_field(key, row_place, col_place):
    wave_count = 6
    length_key = jax.random.fold_in(key, 31)
    turn_key = jax.random.fold_in(key, 32)
    phase_key = jax.random.fold_in(key, 33)
    strength_key = jax.random.fold_in(key, 34)
    lengths = jnp.exp(jax.random.uniform(length_key, (wave_count, NMODE), jnp.float32, math.log(12.0), math.log(96.0)))
    turns = jax.random.uniform(turn_key, (wave_count, NMODE), jnp.float32, 0.0, 2.0 * math.pi)
    phases = jax.random.uniform(phase_key, (wave_count, NMODE), jnp.float32, 0.0, 2.0 * math.pi)
    strengths = jax.random.normal(strength_key, (wave_count, NMODE), jnp.float32) * 0.03
    field = jnp.zeros((NR, NC, NMODE), jnp.float32)
    for wave_index in range(wave_count):
        along_rows = 2.0 * math.pi * jnp.cos(turns[wave_index]) / lengths[wave_index]
        along_cols = 2.0 * math.pi * jnp.sin(turns[wave_index]) / lengths[wave_index]
        angle_field = row_place * along_rows + col_place * along_cols + phases[wave_index]
        field = field + strengths[wave_index] * jnp.cos(angle_field)
    return field


def compact_sources(key, row_place, col_place):
    source_count = 16
    centre_rows = jax.random.randint(jax.random.fold_in(key, 41), (source_count,), 0, NR).astype(jnp.float32)
    centre_cols = jax.random.randint(jax.random.fold_in(key, 42), (source_count,), 0, NC).astype(jnp.float32)
    source_widths = jnp.exp(jax.random.uniform(jax.random.fold_in(key, 43), (source_count,), jnp.float32, math.log(0.8), math.log(2.0)))
    brightness = jnp.exp(jax.random.uniform(jax.random.fold_in(key, 44), (source_count,), jnp.float32, math.log(8.0), math.log(30.0)))
    coefficients = jax.random.normal(jax.random.fold_in(key, 45), (source_count, NMODE), jnp.float32) / math.sqrt(NMODE)
    row_gap = row_place - centre_rows
    col_gap = col_place - centre_cols
    profile = jnp.exp(-(row_gap * row_gap + col_gap * col_gap) / (2.0 * source_widths * source_widths)) * brightness
    return jnp.einsum('rcs,sk->rck', profile, coefficients)


def draw_sky_cube(key, part):
    modes_drawn = sky_modes(key)
    noise_key = jax.random.fold_in(key, 22)
    sigma_key = jax.random.fold_in(key, 23)
    scale_key = jax.random.fold_in(key, 24)
    row_place = jnp.arange(NR, dtype=jnp.int32).astype(jnp.float32)[:, None, None]
    col_place = jnp.arange(NC, dtype=jnp.int32).astype(jnp.float32)[None, :, None]
    amplitudes = diffuse_field(key, row_place, col_place) + compact_sources(key, row_place, col_place)
    noise_field = jax.random.normal(noise_key, (NR, NC, NF), jnp.float32)
    channel_sigma = jnp.exp(jax.random.uniform(sigma_key, (NF,), jnp.float32, math.log(0.03), math.log(0.3)))
    pixel_scale = jnp.exp(jax.random.uniform(scale_key, (NR, NC, 1), jnp.float32, math.log(0.3), math.log(3.0)))
    position = jnp.arange(NR, dtype=jnp.int32).astype(jnp.float32) / NR - 0.5
    row_rise = (3.0 ** position)[:, None, None]
    foreground = jnp.einsum('rck,kf->rcf', amplitudes, modes_drawn)
    values = row_rise * (foreground + channel_sigma[None, None, :] * pixel_scale * noise_field)
    return jnp.clip(values, -40.0, 40.0).astype(jnp.bfloat16)


def draw_half_widths(key, part):
    drawn = jax.random.randint(jax.random.fold_in(key, 3), (NF,), 1, HALF + 1)
    widest = jax.random.randint(jax.random.fold_in(key, 4), (), 0, NF)
    drawn = drawn.at[widest].set(HALF)
    drawn = drawn.at[(widest + 1) % NF].set(1)
    return drawn.astype(jnp.int32)


def set_ends(array, own_key, smallest, high):
    longest = array.shape.index(max(array.shape))
    spots = []
    for shift in (0, 1):
        where = [jax.random.randint(jax.random.fold_in(own_key, axis), (), 0, length) for axis, length in enumerate(array.shape)]
        where[longest] = (where[longest] + shift) % array.shape[longest]
        spots.append(tuple(where))
    return array.at[spots[0]].set(smallest).at[spots[1]].set(high)


def setup_inputs(seed: int = 0, part: int = 0) -> dict:
    arg_keys = jax.random.split(jax.random.key(seed), 5)
    own_keys = jax.random.split(jax.random.fold_in(arg_keys[4], part), 5)
    sky_cube = draw_sky_cube(jax.random.fold_in(jax.random.fold_in(arg_keys[4], part), 71), part)
    half_widths = draw_half_widths(jax.random.fold_in(arg_keys[4], 71), part)
    pixel_mask = set_ends((jax.random.randint(own_keys[2], (NR, NC), 0, 4) < 3).astype(jnp.int32), jax.random.fold_in(own_keys[2], 1), 0, 1)
    foreground_modes = draw_foreground_modes(jax.random.fold_in(jax.random.fold_in(arg_keys[4], part), 71), part)
    return dict(sky_cube=sky_cube, half_widths=half_widths, pixel_mask=pixel_mask, foreground_modes=foreground_modes)


highest = lax.Precision.HIGHEST

def make_taps(half_widths):
    offsets = jnp.arange(2 * HALF + 1, dtype=jnp.int32) - HALF
    distance = offsets.astype(jnp.float32)[:, None]
    spread = half_widths.astype(jnp.float32)[None, :] * 0.5
    inside = jnp.abs(offsets)[:, None] <= half_widths[None, :]
    profile = jnp.where(inside, jnp.exp(-distance * distance / (2.0 * spread * spread)), jnp.float32(0.0))
    return (profile / lax.optimization_barrier(jnp.sum(profile, axis=0, keepdims=True))).astype(jnp.bfloat16)

def window_taper(length):
    angles = 2.0 * math.pi * jnp.arange(length, dtype=jnp.int32).astype(jnp.float32) / (length - 1)
    return 0.35875 - 0.48829 * jnp.cos(angles) + 0.14128 * jnp.cos(2.0 * angles) - 0.01168 * jnp.cos(3.0 * angles)

def dft_table(length):
    indices = jnp.arange(length, dtype=jnp.int32)
    product = indices[:, None] * indices[None, :] % length
    angles = 2.0 * math.pi * product.astype(jnp.float32) / length
    cosine = jnp.cos(angles) / math.sqrt(length)
    sine_part = -jnp.sin(angles) / math.sqrt(length)
    table = jnp.stack([jnp.stack([cosine, -sine_part]), jnp.stack([sine_part, cosine])])
    return table.astype(jnp.bfloat16)

def delay_table():
    channel_index = jnp.arange(NF, dtype=jnp.int32)
    delay_index = jnp.arange(NF // 2, dtype=jnp.int32)
    product = channel_index[:, None] * delay_index[None, :] % NF
    angles = 2.0 * math.pi * product.astype(jnp.float32) / NF
    scale = window_taper(NF)[:, None] / math.sqrt(NF)
    return jnp.stack([jnp.cos(angles) * scale, -jnp.sin(angles) * scale], axis=1).reshape(NF, NF)

def smooth_axis(data, beam_taps, axis):
    length = data.shape[axis]
    widths = [(0, 0), (0, 0), (0, 0)]
    widths[axis] = (HALF, HALF)
    padded = jnp.pad(data, widths)
    taps_wide = beam_taps.astype(jnp.float32)

    def add_tap(tap, running):
        piece = lax.dynamic_slice_in_dim(padded, tap, length, axis)
        return running + taps_wide[tap][None, None, :] * piece
    return lax.fori_loop(0, 2 * HALF + 1, add_tap, jnp.zeros(data.shape, jnp.float32))

def spatial_transform(delay_slab):
    column_table = dft_table(NC).astype(jnp.float32)
    row_table = dft_table(NR).astype(jnp.float32)
    halfway = jnp.einsum('kmrc,nmcd->knrd', delay_slab.astype(jnp.float32), column_table, precision=highest)
    halfway = lax.optimization_barrier(halfway.astype(jnp.bfloat16)).astype(jnp.float32)
    return jnp.einsum('nmsr,kmrd->knsd', row_table, halfway, precision=highest)

def reference(sky_cube, half_widths, pixel_mask, foreground_modes):
    beam_taps = make_taps(half_widths)
    row_smoothed = smooth_axis(sky_cube.astype(jnp.float32), beam_taps, 0).astype(jnp.bfloat16)
    row_smoothed = lax.optimization_barrier(row_smoothed).astype(jnp.float32)
    smoothed = smooth_axis(row_smoothed, beam_taps, 1)
    masked = pixel_mask.astype(jnp.float32)[:, :, None] * smoothed
    power_sum = lax.optimization_barrier(jnp.sum(masked * masked, axis=(0, 1)))
    weights = 1.0 / (power_sum / (NR * NC) + 1e-05)
    channel_weights = weights / jnp.mean(weights)
    weighted_modes = foreground_modes * weights[None, :]
    normal_matrix = jnp.dot(weighted_modes.astype(jnp.float32), foreground_modes.T.astype(jnp.float32), precision=highest, preferred_element_type=jnp.float32)
    pixels = masked.reshape(NR * NC, NF)
    projected = jnp.dot(pixels.astype(jnp.float32), weighted_modes.T.astype(jnp.float32), precision=highest, preferred_element_type=jnp.float32)
    factor = jnp.linalg.cholesky(normal_matrix)
    amplitude = jax.scipy.linalg.cho_solve((factor, True), projected.T)
    cleaned = pixels - jnp.dot(amplitude.T.astype(jnp.float32), foreground_modes.astype(jnp.float32), precision=highest, preferred_element_type=jnp.float32)
    delays = jnp.dot(cleaned.astype(jnp.float32), delay_table().astype(jnp.float32), precision=highest, preferred_element_type=jnp.float32).astype(jnp.bfloat16)
    delay_cube = delays.reshape(NR, NC, 2, NF // 2).transpose(3, 2, 0, 1)

    def one_delay(delay_slab):
        return spatial_transform(delay_slab[None])[0]
    spectrum = lax.map(one_delay, delay_cube)
    return (spectrum, channel_weights)
```

```python
import functools
import math

import jax
import jax.numpy as jnp
from jax import lax
from jax.experimental import pallas as pl
from jax.experimental.pallas import tpu as pltpu
from jax.sharding import PartitionSpec as P

NR = 512
NC = 512
HALF = 16
TAIL = 8


highest = lax.Precision.HIGHEST


def padded(x, sides, width):
    for axis, dim in sides:
        size, length = (lax.axis_size(axis), x.shape[dim])
        up = [(i, (i + 1) % size) for i in range(size - 1)]
        down = [(j, i) for i, j in up]
        last = lax.slice_in_dim(x, length - width, length, axis=dim)
        initial = lax.slice_in_dim(x, 0, width, axis=dim)
        before = lax.ppermute(last, axis, up)
        after = lax.ppermute(initial, axis, down)
        x = jnp.concatenate([before, x, after], axis=dim)
    return x


def make_taps(half_widths):
    offsets = jnp.arange(2 * HALF + 1, dtype=jnp.int32) - HALF
    distance = offsets.astype(jnp.float32)[:, None]
    spread = half_widths.astype(jnp.float32)[None, :] * 0.5
    inside = jnp.abs(offsets)[:, None] <= half_widths[None, :]
    profile = jnp.where(
        inside, jnp.exp(-distance * distance / (2.0 * spread * spread)), jnp.float32(0.0)
    )
    return (profile / jnp.sum(profile, axis=0, keepdims=True)).astype(jnp.bfloat16)


def banded_taps(outputs, beam_taps):
    offsets = (
        jnp.arange(outputs + 2 * HALF, dtype=jnp.int32)[None, :]
        - jnp.arange(outputs, dtype=jnp.int32)[:, None]
    )
    one_hot = (
        offsets[:, :, None] == jnp.arange(2 * HALF + 1, dtype=jnp.int32)[None, None, :]
    ).astype(jnp.bfloat16)
    return jnp.einsum("oit,tf->oif", one_hot, beam_taps, preferred_element_type=jnp.float32).astype(
        jnp.bfloat16
    )


def window_taper(length):
    angles = 2.0 * math.pi * jnp.arange(length, dtype=jnp.int32).astype(jnp.float32) / (length - 1)
    return (
        0.35875
        - 0.48829 * jnp.cos(angles)
        + 0.14128 * jnp.cos(2.0 * angles)
        - 0.01168 * jnp.cos(3.0 * angles)
    )


def dft_table(length):
    indices = jnp.arange(length, dtype=jnp.int32)
    product = indices[:, None] * indices[None, :] % length
    angles = 2.0 * math.pi * product.astype(jnp.float32) / length
    cosine = jnp.cos(angles) / math.sqrt(length)
    sine_part = -jnp.sin(angles) / math.sqrt(length)
    table = jnp.stack([jnp.stack([cosine, -sine_part]), jnp.stack([sine_part, cosine])])
    return table.astype(jnp.bfloat16)


def tile_delay_table(channels, peers):
    per_device = channels // 2 // peers
    slot_index = jnp.arange(channels, dtype=jnp.int32)
    item_index = slot_index // (2 * peers)
    peer_index = slot_index // 2 % peers
    component = slot_index % 2
    delay_index = peer_index * per_device + item_index
    channel_index = jnp.arange(channels, dtype=jnp.int32)
    product = delay_index[:, None] * channel_index[None, :] % channels
    angles = 2.0 * math.pi * product.astype(jnp.float32) / channels
    rows_out = jnp.where(component[:, None] == 0, jnp.cos(angles), -jnp.sin(angles))
    return rows_out * (window_taper(channels) / math.sqrt(channels))[None, :]


def spatial_transform(regrouped):
    items = regrouped.shape[0]
    row_count = lax.axis_size("row")
    col_count = lax.axis_size("col")
    tile_rows = NR // row_count
    tile_cols = NC // col_count
    delay_slab = regrouped.reshape(items, 2, row_count, col_count, tile_rows, tile_cols)
    delay_slab = delay_slab.transpose(0, 1, 2, 4, 3, 5).reshape(items, 2, NR, NC)
    halfway = jnp.einsum(
        "kmrc,nmcd->knrd", delay_slab, dft_table(NC), preferred_element_type=jnp.float32
    )
    halfway = halfway.astype(jnp.bfloat16)
    return jnp.einsum("nmsr,kmrd->knsd", dft_table(NR), halfway, preferred_element_type=jnp.float32)


def body(sky_cube, half_widths, pixel_mask, foreground_modes):
    tile_rows, tile_cols, channels = sky_cube.shape
    beam_taps = make_taps(half_widths)
    row_band = banded_taps(tile_rows, beam_taps)
    extended = padded(sky_cube, (("row", 0),), HALF)
    row_part = jnp.einsum(
        "oif,icf->ocf", row_band, extended, preferred_element_type=jnp.float32
    ).astype(jnp.bfloat16)
    row_smoothed = padded(row_part, (("col", 1),), HALF)
    column_band = banded_taps(tile_cols, beam_taps)
    smoothed = jnp.einsum(
        "oif,rif->rof", column_band, row_smoothed, preferred_element_type=jnp.float32
    )
    masked = pixel_mask.astype(jnp.float32)[:, :, None] * smoothed
    pixels = masked.reshape(tile_rows * tile_cols, channels)
    peers = lax.axis_size("row") * lax.axis_size("col")
    delay_table = tile_delay_table(channels, peers)
    power_sum = lax.psum(jnp.sum(masked * masked, axis=(0, 1)), ("row", "col"))
    weights = 1.0 / (power_sum / (NR * NC) + 1e-05)
    channel_weights = weights / jnp.mean(weights)
    weighted_modes = foreground_modes * weights[None, :]
    normal_matrix = jnp.dot(
        weighted_modes, foreground_modes.T, precision=highest, preferred_element_type=jnp.float32
    )
    projected = jnp.dot(
        pixels, weighted_modes.T, precision=highest, preferred_element_type=jnp.float32
    )
    factor = jnp.linalg.cholesky(normal_matrix)
    amplitude = jax.scipy.linalg.cho_solve((factor, True), projected.T)
    cleaned = pixels - jnp.dot(
        amplitude.T, foreground_modes, precision=highest, preferred_element_type=jnp.float32
    )
    delay_tile = lax.dot_general(
        delay_table,
        cleaned,
        (((1,), (1,)), ((), ())),
        precision=highest,
        preferred_element_type=jnp.float32,
    )
    per_device = channels // 2 // peers
    sendable = delay_tile.astype(jnp.bfloat16).reshape(
        per_device, peers, 2, 1, 1, tile_rows * tile_cols
    )
    spectrum = spatial_transform(
        lax.all_to_all(sendable, ("row", "col"), split_axis=1, concat_axis=3, tiled=True)
    )
    return (spectrum, channel_weights)


FBLOCK = 16
RBLOCK = 16
LANES = 128
MESH = pl.DeviceIdType.MESH


def band_tables(outputs):
    widths = jnp.arange(1, HALF + 1, dtype=jnp.int32)
    spread = widths.astype(jnp.float32) * 0.5
    offsets = jnp.arange(2 * HALF + 1, dtype=jnp.int32) - HALF

    def profile(t, width, spread):
        d = t.astype(jnp.float32)
        return jnp.where(
            jnp.abs(t) <= width, jnp.exp(-d * d / (2.0 * spread * spread)), jnp.float32(0.0)
        )

    total = jnp.sum(profile(offsets[:, None], widths[None, :], spread[None, :]), axis=0)
    place = jnp.concatenate(
        [
            jnp.arange(outputs, dtype=jnp.int32),
            jnp.arange(HALF, dtype=jnp.int32) - HALF,
            jnp.arange(HALF, dtype=jnp.int32) + outputs,
        ]
    )
    t = place[None, None, :] - jnp.arange(outputs, dtype=jnp.int32)[None, :, None]
    w3, s3, n3 = (v[:, None, None] for v in (widths, spread, total))
    return (profile(t, w3, s3) / n3).astype(jnp.bfloat16)


def smooth_kernel(hw_ref, main_ref, rowh_ref, colh_ref, corner_ref, mask_ref, brow_ref, bcol_ref, out_ref, pow_ref, rows_t, cols_t):
    rows, fblock, cols = out_ref.shape
    flat = out_ref.reshape(rows * fblock, cols)
    lanes = rowh_ref.shape[2]
    pitch = lanes + 8
    ring, side = rowh_ref.shape[0], colh_ref.shape[1]
    packs = LANES // side
    lines = (rows + ring) // packs
    sub = pl.program_id(1) * fblock
    base = pl.program_id(0) * lanes + sub

    @pl.when(pl.program_id(1) == 0)
    def _():
        for ref, first in ((main_ref, 0), (rowh_ref, rows)):
            def turn(r, carry):
                start = pl.multiple_of((first + r) * pitch, 8)
                rows_t[pl.ds(start, lanes), :] = ref[r].T.astype(jnp.float32)
                return carry

            lax.fori_loop(0, ref.shape[0], turn, 0, unroll=8)
        for g in range(lines):
            group = [g + lines * p for p in range(packs)]
            group = [colh_ref[r] if r < rows else corner_ref[r - rows] for r in group]
            cols_t[g * pitch : g * pitch + lanes, :] = jnp.concatenate(group, axis=0).T.astype(jnp.float32)

    mask = mask_ref[...]
    for i in range(fblock):
        pick = hw_ref[base + i] - 1
        left = rows_t[pl.ds(sub + i, rows + ring, stride=pitch), :].astype(jnp.bfloat16)
        packed = cols_t[pl.ds(sub + i, lines, stride=pitch), :]
        right = [packed[:, side * p : side * (p + 1)] for p in range(packs)]
        right = jnp.concatenate(right, axis=0).astype(jnp.bfloat16)
        ext = jnp.concatenate([left, right], axis=1)
        part = jnp.dot(brow_ref[pick], ext, preferred_element_type=jnp.float32).astype(jnp.bfloat16)
        done = jnp.dot(part, bcol_ref[pick], preferred_element_type=jnp.float32) * mask
        flat[pl.ds(i, rows, stride=fblock), :] = done
        pow_ref[pl.ds(i, 1), :] = jnp.sum(done * done, axis=0, keepdims=True)


def smooth(half_widths, main, rowh, colh, corner, mask, brow, bcol):
    rows, cols, channels = main.shape
    inner = LANES // FBLOCK
    ring, side = rowh.shape[0], colh.shape[1]
    raw = lambda a: pl.BlockSpec(a.shape[:2] + (LANES,), lambda i, j, hw: (0, 0, i))
    whole = lambda a: pl.BlockSpec(a.shape, lambda i, j, hw: (0,) * a.ndim)
    return pl.pallas_call(
        smooth_kernel,
        grid_spec=pltpu.PrefetchScalarGridSpec(
            num_scalar_prefetch=1,
            grid=(channels // LANES, inner),
            in_specs=[
                raw(main),
                raw(rowh),
                raw(colh),
                raw(corner),
                whole(mask),
                whole(brow),
                whole(bcol),
            ],
            out_specs=[
                pl.BlockSpec((rows, FBLOCK, cols), lambda i, j, hw: (0, i * inner + j, 0)),
                pl.BlockSpec((FBLOCK, cols), lambda i, j, hw: (i * inner + j, 0)),
            ],
            scratch_shapes=[
                pltpu.VMEM(((rows + ring) * (LANES + 8), cols), jnp.float32),
                pltpu.VMEM(((rows + ring) * side // LANES * (LANES + 8), LANES), jnp.float32),
            ],
        ),
        out_shape=[
            jax.ShapeDtypeStruct((rows, channels, cols), jnp.float32),
            jax.ShapeDtypeStruct((channels, cols), jnp.float32),
        ],
        name="smooth",
    )(half_widths, main, rowh, colh, corner, mask, brow, bcol)


def split3(x):
    first = x.astype(jnp.bfloat16)
    rest = x - first.astype(jnp.float32)
    second = rest.astype(jnp.bfloat16)
    third = (rest - second.astype(jnp.float32)).astype(jnp.bfloat16)
    return first, second, third


def outer_split3(x):
    first = lax.reduce_precision(x, 8, 7)
    second = lax.reduce_precision(x - first, 8, 7)
    third = lax.reduce_precision(x - first - second, 8, 7)
    return [v.astype(jnp.bfloat16) for v in (first, second, third)]


def delay_kernel(sizes, merged, masked_ref, fit_ref, modes_ref, table_ref, *refs):
    outs, stage = refs[:-1], refs[-1]
    rblock, channels, cols = masked_ref.shape
    k = fit_ref.shape[0] // 3
    dot = functools.partial(jnp.dot, preferred_element_type=jnp.float32)

    def pair(j, carry):
        x = jnp.concatenate([masked_ref[2 * j], masked_ref[2 * j + 1]], axis=1)
        x1, x2, x3 = split3(x)
        p1 = dot(fit_ref[...], x1)
        p2 = dot(fit_ref[: 2 * k], x2)
        p3 = dot(fit_ref[:k], x3)
        amp = p1[:k] + ((p1[k : 2 * k] + p2[:k]) + (p1[2 * k :] + p2[k:] + p3))
        a1, a2, a3 = split3(amp)
        stack = jnp.concatenate([a1, a2, a1, a2, a3, a1], axis=0)
        cleaned = (x - dot(modes_ref[...], stack)).astype(jnp.bfloat16)
        delays = dot(table_ref[...], cleaned)
        slots = delays.shape[0]
        stage[pl.ds(2 * j, slots, stride=rblock), :] = delays[:, :cols]
        stage[pl.ds(2 * j + 1, slots, stride=rblock), :] = delays[:, cols:]
        return carry

    lax.fori_loop(0, rblock // 2, pair, 0, unroll=2)
    start, slot = 0, 0
    for n, size in enumerate(sizes):
        out = outs[0] if merged else outs[n]
        peers = out.shape[0]
        rows = peers * 2 * size * rblock
        part = stage[start : start + rows, :].astype(jnp.bfloat16)
        out[:, slot : slot + 2 * size] = part.reshape(peers, 2 * size, rblock, cols)
        start += rows
        slot += 2 * size if merged else 0


def clean_delay(masked, fit, modes, table, sizes, peers, first, count, merged):
    channels, cols = masked.shape[1:]
    base = first // RBLOCK
    whole = lambda a: pl.BlockSpec(a.shape, lambda i: (0,) * a.ndim)
    groups = [sum(sizes)] if merged else sizes
    return pl.pallas_call(
        functools.partial(delay_kernel, sizes, merged),
        grid=(count // RBLOCK,),
        in_specs=[
            pl.BlockSpec((RBLOCK, channels, cols), lambda i: (base + i, 0, 0)),
            whole(fit),
            whole(modes),
            whole(table),
        ],
        out_specs=[pl.BlockSpec((peers, 2 * k, RBLOCK, cols), lambda i: (0, 0, i, 0)) for k in groups],
        out_shape=[jax.ShapeDtypeStruct((peers, 2 * k, count, cols), jnp.bfloat16) for k in groups],
        scratch_shapes=[pltpu.VMEM((table.shape[0] * RBLOCK, cols), jnp.float32)],
        cost_estimate=pl.CostEstimate(
            flops=2 * count * cols * channels * (channels + 288),
            bytes_accessed=count * cols * channels * 6,
            transcendentals=0,
        ),
        name="clean_delay",
    )(masked, fit, modes, table)


def solve_kernel(row_count, col_count, pixels, power_ref, modes_ref, fit_ref, scale_ref, mine, gathered, send_sem, recv_sem):
    grp, row, col = lax.axis_index("grp"), lax.axis_index("row"), lax.axis_index("col")
    me = row * col_count + col
    others = []
    for k in range(1, row_count * col_count):
        r = lax.rem(row + k // col_count, row_count)
        c = lax.rem(col + k % col_count, col_count)
        others.append((grp, r, c))
    barrier = pltpu.get_barrier_semaphore()
    for other in others:
        pl.semaphore_signal(barrier, inc=1, device_id=other, device_id_type=MESH)
    own = jnp.sum(jnp.transpose(power_ref[...]), axis=0, keepdims=True)
    own = jnp.broadcast_to(own, mine.shape)
    mine[...] = own
    pl.semaphore_wait(barrier, len(others))
    copies = []
    for k, other in enumerate(others):
        copies.append(
            pltpu.make_async_remote_copy(
                src_ref=mine,
                dst_ref=gathered.at[me],
                send_sem=send_sem.at[k],
                recv_sem=recv_sem.at[k],
                device_id=other,
                device_id_type=MESH,
            )
        )
    for copy in copies:
        copy.start()
    gathered[me] = own
    modes = modes_ref[...]
    for copy in copies:
        copy.wait()
    total = gathered[0]
    for k in range(1, row_count * col_count):
        total = total + gathered[k]
    weights = (1.0 / (total / pixels + 1e-05))[:1]
    channels = weights.shape[1]
    scale_ref[...] = weights / (jnp.sum(weights, axis=1, keepdims=True) / channels)
    fit = modes * weights
    normal = lax.dot_general(
        fit, modes, (((1,), (1,)), ((), ())), precision=highest, preferred_element_type=jnp.float32
    )
    line = lax.broadcasted_iota(jnp.int32, (modes.shape[0], 1), 0)
    for k in range(modes.shape[0]):
        inverse = 1.0 / normal[k : k + 1, k : k + 1]
        factor = normal[:, k : k + 1]
        top = normal[k : k + 1] * inverse
        top_fit = fit[k : k + 1] * inverse
        normal = jnp.where(line == k, top, normal - factor * top)
        fit = jnp.where(line == k, top_fit, fit - factor * top_fit)
    fit_ref[...] = jnp.concatenate(split3(fit), axis=0)


def solve(power, modes, row_count, col_count):
    channels = power.shape[0]
    peers = row_count * col_count
    return pl.pallas_call(
        functools.partial(solve_kernel, row_count, col_count, NR * NC),
        in_specs=[pl.BlockSpec(memory_space=pltpu.VMEM)] * 2,
        out_specs=[pl.BlockSpec(memory_space=pltpu.VMEM)] * 2,
        out_shape=[
            jax.ShapeDtypeStruct((3 * modes.shape[0], channels), jnp.bfloat16),
            jax.ShapeDtypeStruct((1, channels), jnp.float32),
        ],
        scratch_shapes=[
            pltpu.VMEM((8, channels), jnp.float32),
            pltpu.VMEM((peers, 8, channels), jnp.float32),
            pltpu.SemaphoreType.DMA((peers - 1,)),
            pltpu.SemaphoreType.DMA((peers - 1,)),
        ],
        compiler_params=pltpu.CompilerParams(collective_id=0, has_side_effects=True),
        name="solve",
    )(power, modes)


def spatial_kernel(row_count, col_count, inputs, head_ref, data_ref, ctab_ref, rtab_ref, *refs):
    out_ref = refs[inputs - 4]
    nr, nc = out_ref.shape[2:]
    lines = []
    for i in range(row_count):
        for ref in (head_ref, data_ref):
            tiles = [ref[i * col_count + j, m] for m in range(2) for j in range(col_count)]
            lines.append(jnp.concatenate(tiles, axis=1))
    slab = jnp.concatenate(lines, axis=0)
    half = jnp.dot(slab, ctab_ref[...], preferred_element_type=jnp.float32).astype(jnp.bfloat16)
    half = jnp.concatenate([half[:, :nc], half[:, nc:]], axis=0)
    for m in range(2):
        out_ref[0, m] = jnp.dot(
            rtab_ref[m * nr : (m + 1) * nr, :], half, preferred_element_type=jnp.float32
        )


def spatial(head, data, ctab, rtab, before, first, total, row_count, col_count):
    peers, slots, rows, cols = data.shape
    items = slots // 2
    whole = lambda a: pl.BlockSpec(a.shape, lambda i: (0,) * a.ndim)
    nr, nc = rtab.shape[0] // 2, ctab.shape[0] // 2
    in_specs = [
        pl.BlockSpec((peers, 2) + head.shape[2:], lambda i: (0, first + i, 0, 0)),
        pl.BlockSpec((peers, 2, rows, cols), lambda i: (0, i, 0, 0)),
        whole(ctab),
        whole(rtab),
    ]
    out_specs = [pl.BlockSpec((1, 2, nr, nc), lambda i: (first + i, 0, 0, 0))]
    out_shape = [jax.ShapeDtypeStruct((total, 2, nr, nc), jnp.float32)]
    args = [head, data, ctab, rtab]
    alias = {}
    if before is not None:
        alias[len(args)] = 0
        in_specs.append(pl.BlockSpec(memory_space=pl.ANY))
        args.append(before)
    out = pl.pallas_call(
        functools.partial(spatial_kernel, row_count, col_count, len(args)),
        grid=(items,),
        in_specs=in_specs,
        out_specs=out_specs,
        out_shape=out_shape,
        input_output_aliases=alias,
        cost_estimate=pl.CostEstimate(
            flops=items * 8 * (nr * nc * nc + nr * nr * nc),
            bytes_accessed=items * nr * nc * 12,
            transcendentals=0,
        ),
        name="spatial",
    )(*args)
    return out[0]


def halo(x, axis, dim):
    size, length = lax.axis_size(axis), x.shape[dim]
    up = [(i, (i + 1) % size) for i in range(size - 1)]
    down = [(j, i) for i, j in up]
    before = lax.ppermute(lax.slice_in_dim(x, length - HALF, length, axis=dim), axis, up)
    after = lax.ppermute(lax.slice_in_dim(x, 0, HALF, axis=dim), axis, down)
    return jnp.concatenate([before, after], axis=dim)


def chunked_delay_table(channels, peers, sizes):
    per_device = channels // 2 // peers
    delays, first = [], 0
    for size in sizes:
        slot = jnp.arange(2 * size * peers, dtype=jnp.int32)
        delays.append(slot // (2 * size) * per_device + first + slot // 2 % size)
        first += size
    delay = jnp.concatenate(delays)
    component = jnp.arange(channels, dtype=jnp.int32) % 2
    product = delay[:, None] * jnp.arange(channels, dtype=jnp.int32)[None, :] % channels
    angles = 2.0 * math.pi * product.astype(jnp.float32) / channels
    rows_out = jnp.where(component[:, None] == 0, jnp.cos(angles), -jnp.sin(angles))
    return (rows_out * (window_taper(channels) / math.sqrt(channels))[None, :]).astype(jnp.bfloat16)


def tiled_body(sky_cube, half_widths, pixel_mask, foreground_modes):
    tile_rows, tile_cols, channels = sky_cube.shape
    row_count, col_count = lax.axis_size("row"), lax.axis_size("col")
    peers = row_count * col_count
    per_device = channels // 2 // peers
    last = per_device // TAIL
    sizes = [per_device - last, last] if last else [per_device]
    rowh = halo(sky_cube, "row", 0)
    colh = halo(sky_cube, "col", 1)
    corner = halo(rowh, "col", 1)
    brow = band_tables(tile_rows)
    bcol = band_tables(tile_cols).transpose(0, 2, 1)
    masked, power = smooth(
        half_widths,
        sky_cube,
        rowh,
        colh,
        corner,
        pixel_mask.astype(jnp.float32),
        brow,
        bcol,
    )
    fit, channel_weights = solve(power, foreground_modes, row_count, col_count)
    channel_weights = channel_weights.reshape(channels)
    m1, m2, m3 = outer_split3(foreground_modes.T)
    modes = jnp.concatenate([m1, m1, m2, m2, m1, m3], axis=1)
    table = chunked_delay_table(channels, peers, sizes)
    exchange = lambda x: lax.all_to_all(x, ("row", "col"), split_axis=0, concat_axis=0, tiled=True)
    (head,) = clean_delay(masked, fit, modes, table, sizes, peers, 0, RBLOCK, True)
    pieces = clean_delay(masked, fit, modes, table, sizes, peers, RBLOCK, tile_rows - RBLOCK, False)
    head = exchange(head)
    ct, rt = dft_table(NC), dft_table(NR)
    ctab = jnp.concatenate(
        [jnp.concatenate([ct[0, 0], ct[1, 0]], axis=1), jnp.concatenate([ct[0, 1], ct[1, 1]], axis=1)], axis=0
    )
    rtab = jnp.concatenate(
        [jnp.concatenate([rt[0, 0], rt[0, 1]], axis=1), jnp.concatenate([rt[1, 0], rt[1, 1]], axis=1)], axis=0
    )

    spectrum = None
    first = 0
    for piece, size in zip(pieces, sizes):
        spectrum = spatial(head, exchange(piece), ctab, rtab, spectrum, first, per_device, row_count, col_count)
        first += size
    return (spectrum, channel_weights)


def pick_body(sky_cube, *rest):
    rows, cols, channels = sky_cube.shape
    fits = rows % 128 == 0 and cols % 128 == 0 and channels % 128 == 0
    return (tiled_body if fits else body)(sky_cube, *rest)


def solution(mesh):
    return jax.shard_map(
        pick_body,
        mesh=mesh,
        in_specs=(P(("grp", "row"), "col", None), P(), P(("grp", "row"), "col"), P("grp", None)),
        out_specs=(P(("grp", "row", "col"), None, None, None), P("grp")),
        check_vma=False,
    )
```
